32 devices in a mesh: row: 8 (over y, x, core), col: 4 (over z).
Axes of the slice: x: 2, y: 2, z: 4, core: 2. Of those that a mesh axis runs over, the one named last changes fastest.
Arguments:
- trailing: float32 [6144, 4096], P('row', 'col'), may hold values from -6 to 6
- column_block: bfloat16 [6144, 1024], P('row', 'col'), may hold values from -6 to 6
- row_block: bfloat16 [1024, 4096], P('row', 'col'), may hold values from -0.1875 to 0.1875
- lower_inv: bfloat16 [1024, 1024], replicated, may hold values from -1 to 1, as said below
- upper_inv: bfloat16 [1024, 1024], replicated, may hold values from -2 to 2, as said below
Outputs:
- lower_panel: bfloat16 [6144, 1024], P('row', 'col')
- upper_panel: bfloat16 [1024, 4096], P('row', 'col')
- updated: float32 [6144, 4096], P('row', 'col')
The draws below stay inside these ranges and needn't reach their ends.
Inputs may be any that keep to these rules, and one draw needn't show every extreme that they name: `lower_inv`: lower triangular with ones on the diagonal. `upper_inv`: upper triangular with diagonal entries between 0.5 and 2.
All inputs are finite; a program needn't handle non-finite values.
Results may differ from the reference program's by a relative error of at most 0.0044.
Values may be sent and summed in bfloat16 or wider, within the bound.
A program may use at most 64 MiB of HBM per device.

```python
import jax
import jax.numpy as jnp

NB = 1024
WROWS = 6144
WCOLS = 4096


def off_diagonal(key):
    first = jax.random.fold_in(jax.random.fold_in(key, 7), 0)
    values = jax.random.normal(first, (NB, NB), jnp.float32)
    return jnp.clip(values * NB ** (-0.5), -0.25, 0.25)


def draw_lower_inv(key, part):
    rowids = jnp.arange(NB)[:, None]
    colids = jnp.arange(NB)[None, :]
    values = off_diagonal(key)
    result = jnp.where(rowids > colids, values, jnp.where(rowids == colids, 1.0, 0.0))
    return result.astype(jnp.bfloat16)


def draw_upper_inv(key, part):
    rowids = jnp.arange(NB)[:, None]
    colids = jnp.arange(NB)[None, :]
    values = off_diagonal(jax.random.fold_in(key, 3))
    diag_key = jax.random.fold_in(key, 11)
    scales = jnp.exp(jax.random.uniform(diag_key, (NB, 1), jnp.float32, jnp.log(0.5), jnp.log(2.0)))
    result = jnp.where(rowids < colids, values, jnp.where(rowids == colids, scales, 0.0))
    return result.astype(jnp.bfloat16)


def block_levels(own_key, dims, cuts, smallest, largest):
    factor_of = 1.0
    for axis_at, shards_of in cuts:
        steps = jax.random.uniform(jax.random.fold_in(jax.random.fold_in(own_key, 6), axis_at), (shards_of,), jnp.float32, smallest / len(cuts), largest / len(cuts))
        factor_of = factor_of * jnp.repeat(jnp.exp(steps), dims[axis_at] // shards_of).reshape((-1,) + (1,) * (len(dims) - 1 - axis_at))
    return factor_of


def centred(rng, dims, spread, bound, pieces=(), held_as=jnp.bfloat16):
    values = spread * jax.random.normal(rng, dims, jnp.float32)
    if pieces:
        values = values * block_levels(rng, dims, pieces, -0.22, 0.18)
    return jnp.clip(values, -bound, bound).astype(held_as)


def setup_inputs(seed: int = 0) -> dict:
    arg_keys = jax.random.split(jax.random.key(seed), 6)
    return {
        "trailing": centred(arg_keys[0], (WROWS, WCOLS), 1.0, 6.0, ((0, 8), (1, 4)), jnp.float32),
        "column_block": centred(arg_keys[1], (WROWS, NB), 1.0, 6.0, ((0, 8), (1, 4))),
        "row_block": centred(arg_keys[2], (NB, WCOLS), NB ** -0.5, 0.1875, ((0, 8), (1, 4))),
        "lower_inv": draw_lower_inv(jax.random.fold_in(arg_keys[5], 71), 0),
        "upper_inv": draw_upper_inv(jax.random.fold_in(arg_keys[5], 71), 0),
    }


def reference(trailing, column_block, row_block, lower_inv, upper_inv):
    lower_panel = jnp.dot(column_block, upper_inv, preferred_element_type=jnp.float32).astype(jnp.bfloat16)
    upper_panel = jnp.dot(lower_inv, row_block, preferred_element_type=jnp.float32).astype(jnp.bfloat16)
    updated = trailing - jnp.dot(lower_panel, upper_panel, preferred_element_type=jnp.float32)
    return lower_panel, upper_panel, updated
```

```python
import functools

import jax
import jax.numpy as jnp
from jax import lax
from jax.experimental import pallas as pl
from jax.experimental.pallas import tpu as pltpu
from jax.sharding import PartitionSpec as P

MESH = pl.DeviceIdType.MESH
BLOCK = 256
COL_CHUNKS = 6
ROW_CHUNKS = 4
GROUPS = (2, 2, 1, 1)
AHEAD = 2


def reach(size, chunk):
    each = (size - 1) // 2
    extra = 1 if size % 2 == 0 else 0
    return (each + extra, each) if chunk % 2 == 0 else (each, each + extra)


def kernel(
    n_row, n_col,
    trailing, column_block, row_block, lower_inv, upper_inv,
    lower_tile, upper_tile, updated,
    gathered, strips, linv, uinv, lower, upper,
    local_sem, own_sem, col_send, col_recv, row_send, row_recv, sib_send, sib_recv,
):
    rows, share = column_block.shape
    depth, cols = row_block.shape
    order = lower_inv.shape[0]
    tall, wide = rows // COL_CHUNKS, cols // ROW_CHUNKS
    row, col = lax.axis_index("row"), lax.axis_index("col")
    chips = n_row // 2
    half = chips // 2
    core = lax.rem(row, 2)

    def snake(place):
        return place + (place // half) * (chips + half - 1 - 2 * place)

    place = snake(row // 2)

    def chip_at(offset):
        return snake(lax.rem(place + chips + offset, chips))

    sibling = {"row": row + 1 - 2 * core}
    row_next = {"row": chip_at(1) * 2 + core}
    row_prev = {"row": chip_at(-1) * 2 + core}
    col_next = {"col": lax.rem(col + 1, n_col)}
    col_prev = {"col": lax.rem(col + n_col - 1, n_col)}

    load_l = pltpu.make_async_copy(lower_inv, linv, local_sem.at[0])
    load_u = pltpu.make_async_copy(upper_inv, uinv, local_sem.at[1])
    load_t = pltpu.make_async_copy(trailing, updated, local_sem.at[2])
    mine_c = pltpu.make_async_copy(column_block, gathered.at[col], own_sem.at[0])
    my_rows = pl.ds(pl.multiple_of(row * depth, depth), depth)
    mine_r = pltpu.make_async_copy(row_block, strips.at[my_rows], own_sem.at[1])

    barrier = pltpu.get_barrier_semaphore()
    for device in (col_next, col_prev, row_next, row_prev, sibling):
        pl.semaphore_signal(barrier, inc=1, device_id=device, device_id_type=MESH)
    mine_c.start()
    mine_r.start()
    load_l.start()
    load_u.start()
    pl.semaphore_wait(barrier, 5)

    sent = []

    def send(src, dst, send_sem, recv_sem, device):
        copy = pltpu.make_async_remote_copy(
            src_ref=src, dst_ref=dst, send_sem=send_sem, recv_sem=recv_sem,
            device_id=device, device_id_type=MESH,
        )
        copy.start()
        sent.append(copy)

    def arrived(dst, sem):
        pltpu.make_async_copy(dst, dst, sem).wait()

    def col_slot(offset, chunk):
        owner = lax.rem(col + n_col + offset, n_col)
        return gathered.at[owner, pl.ds(chunk * tall, tall)]

    def col_send_to(way, step, chunk, src):
        offset = (1 - step) if way == 0 else (step - 1)
        send(
            src, col_slot(offset, chunk),
            col_send.at[way, step - 1, chunk], col_recv.at[way, step - 1, chunk],
            col_next if way == 0 else col_prev,
        )

    def col_own(chunk):
        src = column_block.at[pl.ds(chunk * tall, tall)]
        for way in range(2):
            if reach(n_col, chunk)[way] >= 1:
                col_send_to(way, 1, chunk, src)

    def col_event(step, chunk):
        for way in range(2):
            limit = reach(n_col, chunk)[way]
            if step <= limit:
                slot = col_slot(-step if way == 0 else step, chunk)
                arrived(slot, col_recv.at[way, step - 1, chunk])
                if step < limit:
                    col_send_to(way, step + 1, chunk, slot)

    def strip(offset, lane, chunk):
        owner = chip_at(offset) * 2 + lane
        start = pl.multiple_of(owner * depth, depth)
        return strips.at[pl.ds(start, depth), pl.ds(chunk * wide, wide)]

    def row_send_to(way, step, chunk, src):
        offset = (1 - step) if way == 0 else (step - 1)
        send(
            src, strip(offset, core, chunk),
            row_send.at[way, step - 1, chunk], row_recv.at[way, step - 1, chunk],
            row_next if way == 0 else row_prev,
        )

    def share_strip(offset, chunk, src):
        at = offset + half
        send(
            src, strip(offset, core, chunk),
            sib_send.at[at, chunk], sib_recv.at[at, chunk], sibling,
        )

    shared = [[] for _ in range(ROW_CHUNKS)]

    def row_own(chunk):
        src = row_block.at[:, pl.ds(chunk * wide, wide)]
        for way in range(2):
            if reach(chips, chunk)[way] >= 1:
                row_send_to(way, 1, chunk, src)
        share_strip(0, chunk, src)
        shared[chunk].append(0)

    def row_event(step, chunk):
        for way in range(2):
            limit = reach(chips, chunk)[way]
            if step <= limit:
                offset = -step if way == 0 else step
                slot = strip(offset, core, chunk)
                arrived(slot, row_recv.at[way, step - 1, chunk])
                if step < limit:
                    row_send_to(way, step + 1, chunk, slot)
                share_strip(offset, chunk, slot)
                shared[chunk].append(offset)

    def row_shared(chunk):
        for offset in shared[chunk]:
            arrived(strip(offset, 1 - core, chunk), sib_recv.at[offset + half, chunk])

    def make_upper(chunk):
        at = pl.ds(chunk * wide, wide)
        for i in range(order // BLOCK):
            end = (i + 1) * BLOCK
            upper[pl.ds(i * BLOCK, BLOCK), at] = jnp.dot(
                linv[pl.ds(i * BLOCK, BLOCK), pl.ds(0, end)],
                strips[pl.ds(0, end), at],
                preferred_element_type=jnp.float32,
            ).astype(jnp.bfloat16)

    def make_lower(first, count):
        at = pl.ds(first * tall, count * tall)
        parts = [gathered[k, at] for k in range(n_col)]
        left = jnp.concatenate(parts, axis=1)
        for j in range(order // BLOCK):
            end = (j + 1) * BLOCK
            lower[at, pl.ds(j * BLOCK, BLOCK)] = jnp.dot(
                left[:, :end],
                uinv[pl.ds(0, end), pl.ds(j * BLOCK, BLOCK)],
                preferred_element_type=jnp.float32,
            ).astype(jnp.bfloat16)
        if share % 128 == 0:
            lower_tile[at] = lower[at, pl.ds(pl.multiple_of(col * share, share), share)]
        else:
            for k in range(n_col):
                @pl.when(col == k)
                def _():
                    lower_tile[at] = lower[at, pl.ds(k * share, share)]

    def subtract(first, count):
        at = pl.ds(first * tall, count * tall)

        @pl.loop(0, cols // BLOCK)
        def _(j):
            across = pl.ds(pl.multiple_of(j * BLOCK, BLOCK), BLOCK)
            updated[at, across] -= jnp.dot(
                lower[at], upper[:, across], preferred_element_type=jnp.float32
            )

    col_depth = max(max(reach(n_col, q)) for q in range(COL_CHUNKS))
    row_depth = max(max(reach(chips, r)) for r in range(ROW_CHUNKS))
    col_ticks = COL_CHUNKS + col_depth - 1
    row_ticks = ROW_CHUNKS + row_depth - 1
    groups, first = [], 0
    for count in GROUPS:
        groups.append((first, count))
        first += count
    for chunk in range(AHEAD):
        col_own(chunk)
        row_own(chunk)
    load_t.start()
    waiting, made_upper = list(groups), 0
    ready, uppers = [], list(range(ROW_CHUNKS))
    waited_inputs = False
    for tick in range(max(col_ticks, row_ticks + 2) + 1):
        for step in range(1, col_depth + 1):
            chunk = tick - (step - 1)
            if 0 <= chunk < COL_CHUNKS:
                col_event(step, chunk)
        for step in range(1, row_depth + 1):
            chunk = tick - (step - 1)
            if 0 <= chunk < ROW_CHUNKS:
                row_event(step, chunk)
        if AHEAD + tick < COL_CHUNKS:
            col_own(AHEAD + tick)
        if AHEAD + tick < ROW_CHUNKS:
            row_own(AHEAD + tick)
        if tick == 0:
            mine_c.wait()
            mine_r.wait()
            load_l.wait()
            load_u.wait()
        chunk = tick - row_depth
        if 0 <= chunk < ROW_CHUNKS:
            row_shared(chunk)
            make_upper(chunk)
            uppers.remove(chunk)
            if not uppers:
                upper_tile[...] = upper[my_rows]
                load_t.wait()
        while waiting and sum(waiting[0]) - 1 + col_depth - 1 <= tick:
            make_lower(*waiting[0])
            ready.append(waiting.pop(0))
        if not uppers:
            while ready:
                subtract(*ready.pop(0))
    assert not waiting and not ready and not uppers
    for copy in sent:
        copy.wait_send()


def on_device(n_row, n_col, trailing, column_block, row_block, lower_inv, upper_inv):
    rows, share = column_block.shape
    depth, cols = row_block.shape
    order = lower_inv.shape[0]
    chips = n_row // 2
    steps, hops = n_col // 2, chips // 2
    narrow = jnp.bfloat16
    anywhere = pl.BlockSpec(memory_space=pltpu.HBM)
    inside = pl.BlockSpec(memory_space=pltpu.VMEM)
    dma = pltpu.SemaphoreType.DMA
    return pl.pallas_call(
        functools.partial(kernel, n_row, n_col),
        out_shape=(
            jax.ShapeDtypeStruct((rows, share), narrow),
            jax.ShapeDtypeStruct((depth, cols), narrow),
            jax.ShapeDtypeStruct((rows, cols), jnp.float32),
        ),
        in_specs=[anywhere] * 5,
        out_specs=(inside,) * 3,
        scratch_shapes=[
            pltpu.VMEM((n_col, rows, share), narrow),
            pltpu.VMEM((order, cols), narrow),
            pltpu.VMEM((order, order), narrow),
            pltpu.VMEM((order, order), narrow),
            pltpu.VMEM((rows, order), narrow),
            pltpu.VMEM((order, cols), narrow),
            dma((3,)),
            dma((2,)),
            dma((2, steps, COL_CHUNKS)),
            dma((2, steps, COL_CHUNKS)),
            dma((2, hops, ROW_CHUNKS)),
            dma((2, hops, ROW_CHUNKS)),
            dma((2 * hops + 1, ROW_CHUNKS)),
            dma((2 * hops + 1, ROW_CHUNKS)),
        ],
        compiler_params=pltpu.CompilerParams(
            collective_id=0, has_side_effects=True, vmem_limit_bytes=32 << 20
        ),
    )(trailing, column_block, row_block, lower_inv, upper_inv)


def solution(mesh):
    specs = P("row", "col")
    return jax.shard_map(
        functools.partial(on_device, mesh.shape["row"], mesh.shape["col"]),
        mesh=mesh,
        in_specs=(specs, specs, specs, P(), P()),
        out_specs=(specs,) * 3,
        check_vma=False,
    )
```

```python
import functools

import jax
import jax.numpy as jnp
from jax import lax
from jax.experimental import pallas as pl
from jax.experimental.pallas import tpu as pltpu
from jax.sharding import PartitionSpec as P

MESH = pl.DeviceIdType.MESH
BLOCK = 256
COL_CHUNKS = 6
ROW_CHUNKS = 4
GROUPS = (2, 2, 1, 1)
AHEAD = 2


def reach(size, chunk):
    each = (size - 1) // 2
    extra = 1 if size % 2 == 0 else 0
    return (each + extra, each) if chunk % 2 == 0 else (each, each + extra)


def kernel(
    n_row, n_col,
    trailing, column_block, row_block, lower_inv, upper_inv,
    lower_tile, upper_tile, updated,
    gathered, strips, linv, uinv, lower, upper,
    local_sem, own_sem, col_send, col_recv, row_send, row_recv, sib_send, sib_recv,
):
    rows, share = column_block.shape
    depth, cols = row_block.shape
    order = lower_inv.shape[0]
    tall, wide = rows // COL_CHUNKS, cols // ROW_CHUNKS
    row, col = lax.axis_index("row"), lax.axis_index("col")
    chips = n_row // 2
    half = chips // 2
    core = lax.rem(row, 2)

    def snake(place):
        return place + (place // half) * (chips + half - 1 - 2 * place)

    place = snake(row // 2)

    def chip_at(offset):
        return snake(lax.rem(place + chips + offset, chips))

    sibling = {"row": row + 1 - 2 * core}
    row_next = {"row": chip_at(1) * 2 + core}
    row_prev = {"row": chip_at(-1) * 2 + core}
    col_next = {"col": lax.rem(col + 1, n_col)}
    col_prev = {"col": lax.rem(col + n_col - 1, n_col)}

    load_l = pltpu.make_async_copy(lower_inv, linv, local_sem.at[0])
    load_u = pltpu.make_async_copy(upper_inv, uinv, local_sem.at[1])
    load_t = pltpu.make_async_copy(trailing, updated, local_sem.at[2])
    mine_c = pltpu.make_async_copy(column_block, gathered.at[col], own_sem.at[0])
    my_rows = pl.ds(pl.multiple_of(row * depth, depth), depth)
    mine_r = pltpu.make_async_copy(row_block, strips.at[my_rows], own_sem.at[1])

    barrier = pltpu.get_barrier_semaphore()
    for device in (col_next, col_prev, row_next, row_prev, sibling):
        pl.semaphore_signal(barrier, inc=1, device_id=device, device_id_type=MESH)
    mine_c.start()
    mine_r.start()
    load_l.start()
    load_u.start()
    pl.semaphore_wait(barrier, 5)

    sent = []

    def send(src, dst, send_sem, recv_sem, device):
        copy = pltpu.make_async_remote_copy(
            src_ref=src, dst_ref=dst, send_sem=send_sem, recv_sem=recv_sem,
            device_id=device, device_id_type=MESH,
        )
        copy.start()
        sent.append(copy)

    def arrived(dst, sem):
        pltpu.make_async_copy(dst, dst, sem).wait()

    def col_slot(offset, chunk):
        owner = lax.rem(col + n_col + offset, n_col)
        return gathered.at[owner, pl.ds(chunk * tall, tall)]

    def col_send_to(way, step, chunk, src):
        offset = (1 - step) if way == 0 else (step - 1)
        send(
            src, col_slot(offset, chunk),
            col_send.at[way, step - 1, chunk], col_recv.at[way, step - 1, chunk],
            col_next if way == 0 else col_prev,
        )

    def col_own(chunk):
        src = column_block.at[pl.ds(chunk * tall, tall)]
        for way in range(2):
            if reach(n_col, chunk)[way] >= 1:
                col_send_to(way, 1, chunk, src)

    def col_event(step, chunk):
        for way in range(2):
            limit = reach(n_col, chunk)[way]
            if step <= limit:
                slot = col_slot(-step if way == 0 else step, chunk)
                arrived(slot, col_recv.at[way, step - 1, chunk])
                if step < limit:
                    col_send_to(way, step + 1, chunk, slot)

    def strip(offset, lane, chunk):
        owner = chip_at(offset) * 2 + lane
        start = pl.multiple_of(owner * depth, depth)
        return strips.at[pl.ds(start, depth), pl.ds(chunk * wide, wide)]

    def row_send_to(way, step, chunk, src):
        offset = (1 - step) if way == 0 else (step - 1)
        send(
            src, strip(offset, core, chunk),
            row_send.at[way, step - 1, chunk], row_recv.at[way, step - 1, chunk],
            row_next if way == 0 else row_prev,
        )

    def share_strip(offset, chunk, src):
        at = offset + half
        send(
            src, strip(offset, core, chunk),
            sib_send.at[at, chunk], sib_recv.at[at, chunk], sibling,
        )

    shared = [[] for _ in range(ROW_CHUNKS)]

    def row_own(chunk):
        src = row_block.at[:, pl.ds(chunk * wide, wide)]
        for way in range(2):
            if reach(chips, chunk)[way] >= 1:
                row_send_to(way, 1, chunk, src)
        share_strip(0, chunk, src)
        shared[chunk].append(0)

    def row_event(step, chunk):
        for way in range(2):
            limit = reach(chips, chunk)[way]
            if step <= limit:
                offset = -step if way == 0 else step
                slot = strip(offset, core, chunk)
                arrived(slot, row_recv.at[way, step - 1, chunk])
                if step < limit:
                    row_send_to(way, step + 1, chunk, slot)
                share_strip(offset, chunk, slot)
                shared[chunk].append(offset)

    def row_shared(chunk):
        for offset in shared[chunk]:
            arrived(strip(offset, 1 - core, chunk), sib_recv.at[offset + half, chunk])

    def make_upper(chunk):
        at = pl.ds(chunk * wide, wide)
        for i in range(order // BLOCK):
            end = (i + 1) * BLOCK
            upper[pl.ds(i * BLOCK, BLOCK), at] = jnp.dot(
                linv[pl.ds(i * BLOCK, BLOCK), pl.ds(0, end)],
                strips[pl.ds(0, end), at],
                preferred_element_type=jnp.float32,
            ).astype(jnp.bfloat16)

    def make_lower(first, count):
        at = pl.ds(first * tall, count * tall)
        parts = [gathered[k, at] for k in range(n_col)]
        left = jnp.concatenate(parts, axis=1)
        for j in range(order // BLOCK):
            end = (j + 1) * BLOCK
            lower[at, pl.ds(j * BLOCK, BLOCK)] = jnp.dot(
                left[:, :end],
                uinv[pl.ds(0, end), pl.ds(j * BLOCK, BLOCK)],
                preferred_element_type=jnp.float32,
            ).astype(jnp.bfloat16)
        if share % 128 == 0:
            lower_tile[at] = lower[at, pl.ds(pl.multiple_of(col * share, share), share)]
        else:
            for k in range(n_col):
                @pl.when(col == k)
                def _():
                    lower_tile[at] = lower[at, pl.ds(k * share, share)]

    def subtract(first, count):
        at = pl.ds(first * tall, count * tall)

        @pl.loop(0, cols // BLOCK)
        def _(j):
            across = pl.ds(pl.multiple_of(j * BLOCK, BLOCK), BLOCK)
            updated[at, across] -= jnp.dot(
                lower[at], upper[:, across], preferred_element_type=jnp.float32
            )

    col_depth = max(max(reach(n_col, q)) for q in range(COL_CHUNKS))
    row_depth = max(max(reach(chips, r)) for r in range(ROW_CHUNKS))
    col_ticks = COL_CHUNKS + col_depth - 1
    row_ticks = ROW_CHUNKS + row_depth - 1
    groups, first = [], 0
    for count in GROUPS:
        groups.append((first, count))
        first += count
    for chunk in range(AHEAD):
        col_own(chunk)
        row_own(chunk)
    load_t.start()
    waiting, made_upper = list(groups), 0
    ready, uppers = [], list(range(ROW_CHUNKS))
    waited_inputs = False
    for tick in range(max(col_ticks, row_ticks + 2) + 1):
        for step in range(1, col_depth + 1):
            chunk = tick - (step - 1)
            if 0 <= chunk < COL_CHUNKS:
                col_event(step, chunk)
        for step in range(1, row_depth + 1):
            chunk = tick - (step - 1)
            if 0 <= chunk < ROW_CHUNKS:
                row_event(step, chunk)
        if AHEAD + tick < COL_CHUNKS:
            col_own(AHEAD + tick)
        if AHEAD + tick < ROW_CHUNKS:
            row_own(AHEAD + tick)
        if tick == 0:
            mine_c.wait()
            mine_r.wait()
            load_l.wait()
            load_u.wait()
        chunk = tick - row_depth
        if 0 <= chunk < ROW_CHUNKS:
            row_shared(chunk)
            make_upper(chunk)
            uppers.remove(chunk)
            if not uppers:
                upper_tile[...] = upper[my_rows]
                load_t.wait()
        while waiting and sum(waiting[0]) - 1 + col_depth - 1 <= tick:
            make_lower(*waiting[0])
            ready.append(waiting.pop(0))
        if not uppers:
            while ready:
                subtract(*ready.pop(0))
    assert not waiting and not ready and not uppers
    for copy in sent:
        copy.wait_send()


def on_device(n_row, n_col, trailing, column_block, row_block, lower_inv, upper_inv):
    rows, share = column_block.shape
    depth, cols = row_block.shape
    order = lower_inv.shape[0]
    chips = n_row // 2
    steps, hops = n_col // 2, chips // 2
    narrow = jnp.bfloat16
    anywhere = pl.BlockSpec(memory_space=pltpu.HBM)
    inside = pl.BlockSpec(memory_space=pltpu.VMEM)
    dma = pltpu.SemaphoreType.DMA
    return pl.pallas_call(
        functools.partial(kernel, n_row, n_col),
        out_shape=(
            jax.ShapeDtypeStruct((rows, share), narrow),
            jax.ShapeDtypeStruct((depth, cols), narrow),
            jax.ShapeDtypeStruct((rows, cols), jnp.float32),
        ),
        in_specs=[anywhere] * 5,
        out_specs=(inside,) * 3,
        scratch_shapes=[
            pltpu.VMEM((n_col, rows, share), narrow),
            pltpu.VMEM((order, cols), narrow),
            pltpu.VMEM((order, order), narrow),
            pltpu.VMEM((order, order), narrow),
            pltpu.VMEM((rows, order), narrow),
            pltpu.VMEM((order, cols), narrow),
            dma((3,)),
            dma((2,)),
            dma((2, steps, COL_CHUNKS)),
            dma((2, steps, COL_CHUNKS)),
            dma((2, hops, ROW_CHUNKS)),
            dma((2, hops, ROW_CHUNKS)),
            dma((2 * hops + 1, ROW_CHUNKS)),
            dma((2 * hops + 1, ROW_CHUNKS)),
        ],
        compiler_params=pltpu.CompilerParams(
            collective_id=0, has_side_effects=True, vmem_limit_bytes=32 << 20
        ),
    )(*(pltpu.with_memory_space_constraint(x, pltpu.HBM) for x in (trailing, column_block, row_block, lower_inv, upper_inv)))


def solution(mesh):
    specs = P("row", "col")
    return jax.shard_map(
        functools.partial(on_device, mesh.shape["row"], mesh.shape["col"]),
        mesh=mesh,
        in_specs=(specs, specs, specs, P(), P()),
        out_specs=(specs,) * 3,
        check_vma=False,
    )
```

```python
import functools

import jax
import jax.numpy as jnp
from jax import lax
from jax.experimental import pallas as pl
from jax.experimental.pallas import tpu as pltpu
from jax.sharding import PartitionSpec as P

MESH = pl.DeviceIdType.MESH
BLOCK = 256
PARTS = (3, 3, 3, 2, 1)
ROW_CHUNKS = 4


def chunks_of(rows):
    unit = rows // sum(PARTS)
    starts = [sum(PARTS[:k]) * unit for k in range(len(PARTS))]
    return [(start, part * unit) for start, part in zip(starts, PARTS)]


def reach(size, chunk):
    each = (size - 1) // 2
    extra = 1 if size % 2 == 0 else 0
    return (each + extra, each) if chunk % 2 == 0 else (each, each + extra)


def kernel(
    n_row, n_col,
    trailing, column_block, row_block, lower_inv, upper_inv,
    lower_tile, lower_last, upper, updated,
    gathered, strips, linv, uinv, lower,
    local_sem, own_sem, col_send, col_recv, row_send, row_recv, sib_send, sib_recv,
):
    rows, share = column_block.shape
    depth, cols = row_block.shape
    order = lower_inv.shape[0]
    pieces = chunks_of(rows)
    wide = cols // ROW_CHUNKS
    row, col = lax.axis_index("row"), lax.axis_index("col")
    chips = n_row // 2
    half = chips // 2
    core = lax.rem(row, 2)

    def snake(place):
        return place + (place // half) * (chips + half - 1 - 2 * place)

    place = snake(row // 2)

    def chip_at(offset):
        return snake(lax.rem(place + chips + offset, chips))

    sibling = {"row": row + 1 - 2 * core}
    row_next = {"row": chip_at(1) * 2 + core}
    row_prev = {"row": chip_at(-1) * 2 + core}
    after = {"col": col + 1}
    before = {"col": col - 1}
    has_after = col < n_col - 1
    has_before = col > 0

    load_l = pltpu.make_async_copy(lower_inv, linv, local_sem.at[0])
    load_u = pltpu.make_async_copy(upper_inv, uinv, local_sem.at[1])
    load_t = pltpu.make_async_copy(trailing, updated, local_sem.at[2])
    mine_c = pltpu.make_async_copy(column_block, gathered.at[col], own_sem.at[0])
    my_rows = pl.ds(pl.multiple_of(row * depth, depth), depth)
    mine_r = pltpu.make_async_copy(row_block, strips.at[my_rows], own_sem.at[1])

    barrier = pltpu.get_barrier_semaphore()

    def greet(device):
        pl.semaphore_signal(barrier, inc=1, device_id=device, device_id_type=MESH)

    pl.when(has_after)(lambda: greet(after))
    pl.when(has_before)(lambda: greet(before))
    for device in (row_next, row_prev, sibling):
        greet(device)
    mine_c.start()
    mine_r.start()
    load_l.start()
    load_u.start()
    ahead = (2 * n_col - 3 - col) // (n_col - 1)
    behind = (n_col - 2 + col) // (n_col - 1)
    pl.semaphore_wait(barrier, 3 + ahead + behind)

    sent = []

    def send(src, dst, send_sem, recv_sem, device):
        copy = pltpu.make_async_remote_copy(
            src_ref=src, dst_ref=dst, send_sem=send_sem, recv_sem=recv_sem,
            device_id=device, device_id_type=MESH,
        )
        copy.start()
        sent.append(copy)

    def arrived(dst, sem):
        pltpu.make_async_copy(dst, dst, sem).wait()

    def col_slot(owner, chunk):
        return gathered.at[owner, pl.ds(*pieces[chunk])]

    def col_copy(way, step, chunk):
        owner = col + (1 - step if way == 0 else step - 1)
        slot = col_slot(owner, chunk)
        return pltpu.make_async_remote_copy(
            src_ref=column_block.at[pl.ds(*pieces[chunk])] if step == 1 else slot,
            dst_ref=slot,
            send_sem=col_send.at[way, step - 1, chunk],
            recv_sem=col_recv.at[way, step - 1, chunk],
            device_id=after if way == 0 else before,
            device_id_type=MESH,
        )

    def sends(way, step):
        if way == 0:
            return has_after if step == 1 else has_after & (col >= step - 1)
        return has_before if step == 1 else has_before & (col + step - 1 < n_col)

    def takes(way, step):
        return col >= step if way == 0 else col + step < n_col

    def col_own(way):
        @pl.when(sends(way, 1))
        def _():
            for chunk in range(len(pieces)):
                col_copy(way, 1, chunk).start()

    def col_event(step, chunk):
        for way in range(2):
            @pl.when(takes(way, step))
            def _():
                slot = col_slot(col - step if way == 0 else col + step, chunk)
                arrived(slot, col_recv.at[way, step - 1, chunk])

            if step < n_col - 1:
                @pl.when(sends(way, step + 1))
                def _():
                    col_copy(way, step + 1, chunk).start()

    def col_drain():
        for way in range(2):
            for step in range(1, n_col):
                @pl.when(sends(way, step))
                def _():
                    for chunk in range(len(pieces)):
                        col_copy(way, step, chunk).wait_send()

    def strip(offset, lane, chunk):
        owner = chip_at(offset) * 2 + lane
        start = pl.multiple_of(owner * depth, depth)
        return strips.at[pl.ds(start, depth), pl.ds(chunk * wide, wide)]

    def row_send_to(way, step, chunk, src):
        offset = (1 - step) if way == 0 else (step - 1)
        send(
            src, strip(offset, core, chunk),
            row_send.at[way, step - 1, chunk], row_recv.at[way, step - 1, chunk],
            row_next if way == 0 else row_prev,
        )

    def share_strip(offset, chunk, src):
        at = offset + half
        send(
            src, strip(offset, core, chunk),
            sib_send.at[at, chunk], sib_recv.at[at, chunk], sibling,
        )

    shared = [[] for _ in range(ROW_CHUNKS)]

    def row_own(chunk):
        src = row_block.at[:, pl.ds(chunk * wide, wide)]
        for way in range(2):
            if reach(chips, chunk)[way] >= 1:
                row_send_to(way, 1, chunk, src)
        share_strip(0, chunk, src)
        shared[chunk].append(0)

    def row_event(step, chunk):
        for way in range(2):
            limit = reach(chips, chunk)[way]
            if step <= limit:
                offset = -step if way == 0 else step
                slot = strip(offset, core, chunk)
                arrived(slot, row_recv.at[way, step - 1, chunk])
                if step < limit:
                    row_send_to(way, step + 1, chunk, slot)
                share_strip(offset, chunk, slot)
                shared[chunk].append(offset)

    def row_shared(chunk):
        for offset in shared[chunk]:
            arrived(strip(offset, 1 - core, chunk), sib_recv.at[offset + half, chunk])

    def make_upper(chunk):
        at = pl.ds(chunk * wide, wide)
        for i in range(order // BLOCK):
            end = (i + 1) * BLOCK
            upper[pl.ds(i * BLOCK, BLOCK), at] = jnp.dot(
                linv[pl.ds(i * BLOCK, BLOCK), pl.ds(0, end)],
                strips[pl.ds(0, end), at],
                preferred_element_type=jnp.float32,
            ).astype(jnp.bfloat16)

    def make_lower(chunk):
        at = pl.ds(*pieces[chunk])
        parts = [gathered[k, at] for k in range(n_col)]
        left = jnp.concatenate(parts, axis=1)
        for j in range(order // BLOCK):
            end = (j + 1) * BLOCK
            lower[at, pl.ds(j * BLOCK, BLOCK)] = jnp.dot(
                left[:, :end],
                uinv[pl.ds(0, end), pl.ds(j * BLOCK, BLOCK)],
                preferred_element_type=jnp.float32,
            ).astype(jnp.bfloat16)
        if share % 128 == 0:
            lower_tile[at] = lower[at, pl.ds(pl.multiple_of(col * share, share), share)]
        else:
            for k in range(n_col):
                @pl.when(col == k)
                def _():
                    lower_tile[at] = lower[at, pl.ds(k * share, share)]
        if chunk == len(pieces) - 1:
            lower_last[...] = lower[at]

    def subtract(chunk):
        at = pl.ds(*pieces[chunk])

        @pl.loop(0, cols // BLOCK)
        def _(j):
            across = pl.ds(pl.multiple_of(j * BLOCK, BLOCK), BLOCK)
            updated[at, across] -= jnp.dot(
                lower[at], upper[:, across], preferred_element_type=jnp.float32
            )

    col_own(0)
    col_own(1)
    for chunk in range(ROW_CHUNKS):
        row_own(chunk)
    load_t.start()
    row_depth = max(max(reach(chips, r)) for r in range(ROW_CHUNKS))
    last = len(pieces) - 1
    for chunk in range(max(len(pieces), ROW_CHUNKS)):
        if chunk < ROW_CHUNKS:
            row_event(1, chunk)
        if chunk <= last:
            col_event(1, chunk)
    for step in range(2, row_depth + 1):
        for chunk in range(ROW_CHUNKS):
            row_event(step, chunk)
    mine_c.wait()
    mine_r.wait()
    load_l.wait()
    load_u.wait()
    for chunk in range(ROW_CHUNKS):
        row_shared(chunk)
        make_upper(chunk)
    load_t.wait()
    for step in range(2, n_col - 1):
        for chunk in range(len(pieces)):
            col_event(step, chunk)
    for chunk in range(len(pieces)):
        col_event(n_col - 1, chunk)
        make_lower(chunk)
        if chunk < last:
            subtract(chunk)
    for copy in sent:
        copy.wait_send()
    col_drain()


def finish(lower_last, lower_done, upper, partial, lower_tile, upper_tile, updated, rest, sem):
    rows, cols = partial.shape
    depth = upper_tile.shape[0]
    start = pl.multiple_of(lax.axis_index("row") * depth, depth)
    pieces = chunks_of(rows)
    at = pl.ds(*pieces[-1])
    copies = [
        pltpu.make_async_copy(partial.at[pl.ds(*piece)], updated.at[pl.ds(*piece)], sem.at[k])
        for k, piece in enumerate(pieces[:-1])
    ]
    copies.append(pltpu.make_async_copy(lower_done, lower_tile, sem.at[len(pieces)]))
    copies.append(
        pltpu.make_async_copy(upper.at[pl.ds(start, depth)], upper_tile, sem.at[len(pieces) + 1])
    )
    for copy in copies:
        copy.start()
    for j in range(cols // BLOCK):
        across = pl.ds(j * BLOCK, BLOCK)
        rest[:, across] = partial[at, across] - jnp.dot(
            lower_last[...], upper[:, across], preferred_element_type=jnp.float32
        )
    tail = pltpu.make_async_copy(rest, updated.at[at], sem.at[len(pieces) - 1])
    tail.start()
    for copy in copies:
        copy.wait()
    tail.wait()


def on_device(n_row, n_col, trailing, column_block, row_block, lower_inv, upper_inv):
    rows, share = column_block.shape
    depth, cols = row_block.shape
    order = lower_inv.shape[0]
    chips = n_row // 2
    hops = chips // 2
    narrow = jnp.bfloat16
    hbm = pl.BlockSpec(memory_space=pltpu.HBM)
    inside = pl.BlockSpec(memory_space=pltpu.VMEM)
    dma = pltpu.SemaphoreType.DMA
    count = len(PARTS)
    last = chunks_of(rows)[-1][1]
    inputs = (trailing, column_block, row_block, lower_inv, upper_inv)
    tile = jax.ShapeDtypeStruct((rows, share), narrow)
    whole = jax.ShapeDtypeStruct((rows, cols), jnp.float32)
    lower_done, lower_last, upper, partial = pl.pallas_call(
        functools.partial(kernel, n_row, n_col),
        out_shape=(
            tile,
            jax.ShapeDtypeStruct((last, order), narrow),
            jax.ShapeDtypeStruct((order, cols), narrow),
            whole,
        ),
        in_specs=[hbm] * 5,
        out_specs=(inside,) * 4,
        scratch_shapes=[
            pltpu.VMEM((n_col, rows, share), narrow),
            pltpu.VMEM((order, cols), narrow),
            pltpu.VMEM((order, order), narrow),
            pltpu.VMEM((order, order), narrow),
            pltpu.VMEM((rows, order), narrow),
            dma((3,)),
            dma((2,)),
            dma((2, n_col - 1, count)),
            dma((2, n_col - 1, count)),
            dma((2, hops, ROW_CHUNKS)),
            dma((2, hops, ROW_CHUNKS)),
            dma((2 * hops + 1, ROW_CHUNKS)),
            dma((2 * hops + 1, ROW_CHUNKS)),
        ],
        compiler_params=pltpu.CompilerParams(
            collective_id=0, has_side_effects=True, vmem_limit_bytes=32 << 20
        ),
    )(*(pltpu.with_memory_space_constraint(x, pltpu.HBM) for x in inputs))
    return pl.pallas_call(
        finish,
        out_shape=(tile, jax.ShapeDtypeStruct((depth, cols), narrow), whole),
        in_specs=[inside] * 4,
        out_specs=(hbm,) * 3,
        scratch_shapes=[pltpu.VMEM((last, cols), jnp.float32), dma((count + 2,))],
        compiler_params=pltpu.CompilerParams(vmem_limit_bytes=16 << 20),
    )(lower_last, lower_done, upper, partial)


def solution(mesh):
    specs = P("row", "col")
    return jax.shard_map(
        functools.partial(on_device, mesh.shape["row"], mesh.shape["col"]),
        mesh=mesh,
        in_specs=(specs, specs, specs, P(), P()),
        out_specs=(specs,) * 3,
        check_vma=False,
    )
```

```python
import functools

import jax
import jax.numpy as jnp
from jax import lax
from jax.experimental import pallas as pl
from jax.experimental.pallas import tpu as pltpu
from jax.sharding import PartitionSpec as P

MESH = pl.DeviceIdType.MESH
BLOCK = 256
PARTS = (2, 2, 2, 2, 2, 2)
ROW_CHUNKS = 4


def chunks_of(rows):
    unit = rows // sum(PARTS)
    starts = [sum(PARTS[:k]) * unit for k in range(len(PARTS))]
    return [(start, part * unit) for start, part in zip(starts, PARTS)]


def reach(size, chunk):
    each = (size - 1) // 2
    extra = 1 if size % 2 == 0 else 0
    return (each + extra, each) if chunk % 2 == 0 else (each, each + extra)


def kernel(
    n_row, n_col,
    trailing, column_block, row_block, lower_inv, upper_inv,
    lower_tile, lower_last, upper, updated,
    gathered, strips, linv, uinv, lower,
    local_sem, own_sem, col_send, col_recv, row_send, row_recv, sib_send, sib_recv, met,
):
    rows, share = column_block.shape
    depth, cols = row_block.shape
    order = lower_inv.shape[0]
    pieces = chunks_of(rows)
    wide = cols // ROW_CHUNKS
    row, col = lax.axis_index("row"), lax.axis_index("col")
    chips = n_row // 2
    half = chips // 2
    core = lax.rem(row, 2)

    def snake(place):
        return place + (place // half) * (chips + half - 1 - 2 * place)

    place = snake(row // 2)

    def chip_at(offset):
        return snake(lax.rem(place + chips + offset, chips))

    sibling = {"row": row + 1 - 2 * core}
    row_next = {"row": chip_at(1) * 2 + core}
    row_prev = {"row": chip_at(-1) * 2 + core}
    after = {"col": col + 1}
    before = {"col": col - 1}
    has_after = col < n_col - 1
    has_before = col > 0

    load_l = pltpu.make_async_copy(lower_inv, linv, local_sem.at[0])
    load_u = pltpu.make_async_copy(upper_inv, uinv, local_sem.at[1])
    load_t = pltpu.make_async_copy(trailing, updated, local_sem.at[2])
    mine_c = pltpu.make_async_copy(column_block, gathered.at[col], own_sem.at[0])
    my_rows = pl.ds(pl.multiple_of(row * depth, depth), depth)
    mine_r = pltpu.make_async_copy(row_block, strips.at[my_rows], own_sem.at[1])

    barrier = pltpu.get_barrier_semaphore()

    def greet(device):
        pl.semaphore_signal(barrier, inc=1, device_id=device, device_id_type=MESH)

    pl.when(has_after)(lambda: greet(after))
    pl.when(has_before)(lambda: greet(before))
    greet(row_next)
    greet(row_prev)
    pl.when(core == 0)(lambda: greet(sibling))
    mine_c.start()
    mine_r.start()
    load_l.start()
    load_u.start()
    ahead = (2 * n_col - 3 - col) // (n_col - 1)
    behind = (n_col - 2 + col) // (n_col - 1)
    pl.semaphore_wait(barrier, 2 + core + ahead + behind)

    @pl.when(core == 1)
    def _():
        pl.semaphore_signal(met, inc=1, device_id=sibling, device_id_type=MESH)


    sent = []

    def send(src, dst, send_sem, recv_sem, device):
        copy = pltpu.make_async_remote_copy(
            src_ref=src, dst_ref=dst, send_sem=send_sem, recv_sem=recv_sem,
            device_id=device, device_id_type=MESH,
        )
        copy.start()
        sent.append(copy)

    def arrived(dst, sem):
        pltpu.make_async_copy(dst, dst, sem).wait()

    def col_slot(owner, chunk):
        return gathered.at[owner, pl.ds(*pieces[chunk])]

    def col_copy(way, step, chunk):
        owner = col + (1 - step if way == 0 else step - 1)
        slot = col_slot(owner, chunk)
        return pltpu.make_async_remote_copy(
            src_ref=column_block.at[pl.ds(*pieces[chunk])] if step == 1 else slot,
            dst_ref=slot,
            send_sem=col_send.at[way, step - 1, chunk],
            recv_sem=col_recv.at[way, step - 1, chunk],
            device_id=after if way == 0 else before,
            device_id_type=MESH,
        )

    def sends(way, step):
        if way == 0:
            return has_after if step == 1 else has_after & (col >= step - 1)
        return has_before if step == 1 else has_before & (col + step - 1 < n_col)

    def takes(way, step):
        return col >= step if way == 0 else col + step < n_col

    def col_own(way):
        @pl.when(sends(way, 1))
        def _():
            for chunk in range(len(pieces)):
                col_copy(way, 1, chunk).start()

    def col_event(step, chunk):
        for way in range(2):
            @pl.when(takes(way, step))
            def _():
                slot = col_slot(col - step if way == 0 else col + step, chunk)
                arrived(slot, col_recv.at[way, step - 1, chunk])

            if step < n_col - 1:
                @pl.when(sends(way, step + 1))
                def _():
                    col_copy(way, step + 1, chunk).start()

    def col_drain():
        for way in range(2):
            for step in range(1, n_col):
                @pl.when(sends(way, step))
                def _():
                    for chunk in range(len(pieces)):
                        col_copy(way, step, chunk).wait_send()

    def strip(offset, lane, chunk):
        owner = chip_at(offset) * 2 + lane
        start = pl.multiple_of(owner * depth, depth)
        return strips.at[pl.ds(start, depth), pl.ds(chunk * wide, wide)]

    def row_send_to(way, step, chunk, src):
        offset = (1 - step) if way == 0 else (step - 1)
        send(
            src, strip(offset, core, chunk),
            row_send.at[way, step - 1, chunk], row_recv.at[way, step - 1, chunk],
            row_next if way == 0 else row_prev,
        )

    def share_strip(offset, chunk, src):
        at = offset + half
        send(
            src, strip(offset, core, chunk),
            sib_send.at[at, chunk], sib_recv.at[at, chunk], sibling,
        )

    shared = [[] for _ in range(ROW_CHUNKS)]

    def row_own(chunk):
        src = row_block.at[:, pl.ds(chunk * wide, wide)]
        for way in range(2):
            if reach(chips, chunk)[way] >= 1:
                row_send_to(way, 1, chunk, src)

    def row_event(step, chunk):
        for way in range(2):
            limit = reach(chips, chunk)[way]
            if step <= limit:
                offset = -step if way == 0 else step
                slot = strip(offset, core, chunk)
                arrived(slot, row_recv.at[way, step - 1, chunk])
                if step < limit:
                    row_send_to(way, step + 1, chunk, slot)
                share_strip(offset, chunk, slot)
                shared[chunk].append(offset)

    def row_shared(chunk):
        for offset in shared[chunk]:
            arrived(strip(offset, 1 - core, chunk), sib_recv.at[offset + half, chunk])

    def make_upper(chunk):
        at = pl.ds(chunk * wide, wide)
        for i in range(order // BLOCK):
            end = (i + 1) * BLOCK
            upper[pl.ds(i * BLOCK, BLOCK), at] = jnp.dot(
                linv[pl.ds(i * BLOCK, BLOCK), pl.ds(0, end)],
                strips[pl.ds(0, end), at],
                preferred_element_type=jnp.float32,
            ).astype(jnp.bfloat16)

    def make_lower(chunk):
        at = pl.ds(*pieces[chunk])
        parts = [gathered[k, at] for k in range(n_col)]
        left = jnp.concatenate(parts, axis=1)
        for j in range(order // BLOCK):
            end = (j + 1) * BLOCK
            lower[at, pl.ds(j * BLOCK, BLOCK)] = jnp.dot(
                left[:, :end],
                uinv[pl.ds(0, end), pl.ds(j * BLOCK, BLOCK)],
                preferred_element_type=jnp.float32,
            ).astype(jnp.bfloat16)
        if share % 128 == 0:
            lower_tile[at] = lower[at, pl.ds(pl.multiple_of(col * share, share), share)]
        else:
            for k in range(n_col):
                @pl.when(col == k)
                def _():
                    lower_tile[at] = lower[at, pl.ds(k * share, share)]
        if chunk == len(pieces) - 1:
            lower_last[...] = lower[at]

    def subtract(chunk):
        at = pl.ds(*pieces[chunk])

        @pl.loop(0, cols // BLOCK)
        def _(j):
            across = pl.ds(pl.multiple_of(j * BLOCK, BLOCK), BLOCK)
            updated[at, across] -= jnp.dot(
                lower[at], upper[:, across], preferred_element_type=jnp.float32
            )

    col_own(0)
    col_own(1)
    for chunk in range(ROW_CHUNKS):
        row_own(chunk)
    load_t.start()
    pl.when(core == 0)(lambda: pl.semaphore_wait(met, 1))
    for chunk in range(ROW_CHUNKS):
        share_strip(0, chunk, row_block.at[:, pl.ds(chunk * wide, wide)])
        shared[chunk].append(0)
    row_depth = max(max(reach(chips, r)) for r in range(ROW_CHUNKS))
    last = len(pieces) - 1
    for chunk in range(max(len(pieces), ROW_CHUNKS)):
        if chunk < ROW_CHUNKS:
            row_event(1, chunk)
        if chunk <= last:
            col_event(1, chunk)
    for step in range(2, row_depth + 1):
        for chunk in range(ROW_CHUNKS):
            row_event(step, chunk)
    mine_c.wait()
    mine_r.wait()
    load_l.wait()
    load_u.wait()
    for chunk in range(ROW_CHUNKS):
        row_shared(chunk)
        make_upper(chunk)
    load_t.wait()
    for step in range(2, n_col - 1):
        for chunk in range(len(pieces)):
            col_event(step, chunk)
    for chunk in range(len(pieces)):
        col_event(n_col - 1, chunk)
        make_lower(chunk)
        if chunk < last:
            subtract(chunk)
    for copy in sent:
        copy.wait_send()
    col_drain()


def finish(lower_last, lower_done, upper, partial, lower_tile, upper_tile, updated, rest, sem):
    rows, cols = partial.shape
    depth = upper_tile.shape[0]
    start = pl.multiple_of(lax.axis_index("row") * depth, depth)
    pieces = chunks_of(rows)
    at = pl.ds(*pieces[-1])
    copies = [
        pltpu.make_async_copy(partial.at[pl.ds(*piece)], updated.at[pl.ds(*piece)], sem.at[k])
        for k, piece in enumerate(pieces[:-1])
    ]
    copies.append(pltpu.make_async_copy(lower_done, lower_tile, sem.at[len(pieces)]))
    copies.append(
        pltpu.make_async_copy(upper.at[pl.ds(start, depth)], upper_tile, sem.at[len(pieces) + 1])
    )
    for copy in copies:
        copy.start()
    for j in range(cols // BLOCK):
        across = pl.ds(j * BLOCK, BLOCK)
        rest[:, across] = partial[at, across] - jnp.dot(
            lower_last[...], upper[:, across], preferred_element_type=jnp.float32
        )
    tail = pltpu.make_async_copy(rest, updated.at[at], sem.at[len(pieces) - 1])
    tail.start()
    for copy in copies:
        copy.wait()
    tail.wait()


def on_device(n_row, n_col, trailing, column_block, row_block, lower_inv, upper_inv):
    rows, share = column_block.shape
    depth, cols = row_block.shape
    order = lower_inv.shape[0]
    chips = n_row // 2
    hops = chips // 2
    narrow = jnp.bfloat16
    hbm = pl.BlockSpec(memory_space=pltpu.HBM)
    inside = pl.BlockSpec(memory_space=pltpu.VMEM)
    dma = pltpu.SemaphoreType.DMA
    count = len(PARTS)
    last = chunks_of(rows)[-1][1]
    inputs = (trailing, column_block, row_block, lower_inv, upper_inv)
    tile = jax.ShapeDtypeStruct((rows, share), narrow)
    whole = jax.ShapeDtypeStruct((rows, cols), jnp.float32)
    lower_done, lower_last, upper, partial = pl.pallas_call(
        functools.partial(kernel, n_row, n_col),
        out_shape=(
            tile,
            jax.ShapeDtypeStruct((last, order), narrow),
            jax.ShapeDtypeStruct((order, cols), narrow),
            whole,
        ),
        in_specs=[hbm] * 5,
        out_specs=(inside,) * 4,
        scratch_shapes=[
            pltpu.VMEM((n_col, rows, share), narrow),
            pltpu.VMEM((order, cols), narrow),
            pltpu.VMEM((order, order), narrow),
            pltpu.VMEM((order, order), narrow),
            pltpu.VMEM((rows, order), narrow),
            dma((3,)),
            dma((2,)),
            dma((2, n_col - 1, count)),
            dma((2, n_col - 1, count)),
            dma((2, hops, ROW_CHUNKS)),
            dma((2, hops, ROW_CHUNKS)),
            dma((2 * hops + 1, ROW_CHUNKS)),
            dma((2 * hops + 1, ROW_CHUNKS)),
            pltpu.SemaphoreType.REGULAR,
        ],
        compiler_params=pltpu.CompilerParams(
            collective_id=0, has_side_effects=True, vmem_limit_bytes=32 << 20
        ),
    )(*(pltpu.with_memory_space_constraint(x, pltpu.HBM) for x in inputs))
    return pl.pallas_call(
        finish,
        out_shape=(tile, jax.ShapeDtypeStruct((depth, cols), narrow), whole),
        in_specs=[inside] * 4,
        out_specs=(hbm,) * 3,
        scratch_shapes=[pltpu.VMEM((last, cols), jnp.float32), dma((count + 2,))],
        compiler_params=pltpu.CompilerParams(vmem_limit_bytes=16 << 20),
    )(lower_last, lower_done, upper, partial)


def solution(mesh):
    specs = P("row", "col")
    return jax.shard_map(
        functools.partial(on_device, mesh.shape["row"], mesh.shape["col"]),
        mesh=mesh,
        in_specs=(specs, specs, specs, P(), P()),
        out_specs=(specs,) * 3,
        check_vma=False,
    )
```

```python
import functools

import jax
import jax.numpy as jnp
from jax import lax
from jax.experimental import pallas as pl
from jax.experimental.pallas import tpu as pltpu
from jax.sharding import PartitionSpec as P

MESH = pl.DeviceIdType.MESH
BLOCK = 256
TILE = 1024
PARTS = (3, 3, 3, 3)
ROW_CHUNKS = 4


def chunks_of(rows):
    unit = rows // sum(PARTS)
    starts = [sum(PARTS[:k]) * unit for k in range(len(PARTS))]
    return [(start, part * unit) for start, part in zip(starts, PARTS)]


def reach(size, chunk):
    each = (size - 1) // 2
    extra = 1 if size % 2 == 0 else 0
    return (each + extra, each) if chunk % 2 == 0 else (each, each + extra)


def kernel(
    n_row, n_col,
    trailing, column_block, row_block, lower_inv, upper_inv,
    lower_tile, lower_last, upper, updated,
    gathered, strips, linv, uinv, lower,
    local_sem, own_sem, col_send, col_recv, row_send, row_recv, sib_send, sib_recv, met,
):
    rows, share = column_block.shape
    depth, cols = row_block.shape
    order = lower_inv.shape[0]
    pieces = chunks_of(rows)
    wide = cols // ROW_CHUNKS
    row, col = lax.axis_index("row"), lax.axis_index("col")
    chips = n_row // 2
    half = chips // 2
    core = lax.rem(row, 2)

    def snake(place):
        return place + (place // half) * (chips + half - 1 - 2 * place)

    place = snake(row // 2)

    def chip_at(offset):
        return snake(lax.rem(place + chips + offset, chips))

    sibling = {"row": row + 1 - 2 * core}
    row_next = {"row": chip_at(1) * 2 + core}
    row_prev = {"row": chip_at(-1) * 2 + core}
    after = {"col": col + 1}
    before = {"col": col - 1}
    has_after = col < n_col - 1
    has_before = col > 0

    load_l = pltpu.make_async_copy(lower_inv, linv, local_sem.at[0])
    load_u = pltpu.make_async_copy(upper_inv, uinv, local_sem.at[1])
    load_t = pltpu.make_async_copy(trailing, updated, local_sem.at[2])
    mine_c = pltpu.make_async_copy(column_block, gathered.at[col], own_sem.at[0])
    my_rows = pl.ds(pl.multiple_of(row * depth, depth), depth)
    mine_r = pltpu.make_async_copy(row_block, strips.at[my_rows], own_sem.at[1])

    barrier = pltpu.get_barrier_semaphore()

    def greet(device):
        pl.semaphore_signal(barrier, inc=1, device_id=device, device_id_type=MESH)

    pl.when(has_after)(lambda: greet(after))
    pl.when(has_before)(lambda: greet(before))
    greet(row_next)
    greet(row_prev)
    pl.when(core == 0)(lambda: greet(sibling))
    mine_c.start()
    mine_r.start()
    load_l.start()
    load_u.start()
    ahead = (2 * n_col - 3 - col) // (n_col - 1)
    behind = (n_col - 2 + col) // (n_col - 1)
    pl.semaphore_wait(barrier, 2 + core + ahead + behind)

    @pl.when(core == 1)
    def _():
        pl.semaphore_signal(met, inc=1, device_id=sibling, device_id_type=MESH)


    sent = []

    def send(src, dst, send_sem, recv_sem, device):
        copy = pltpu.make_async_remote_copy(
            src_ref=src, dst_ref=dst, send_sem=send_sem, recv_sem=recv_sem,
            device_id=device, device_id_type=MESH,
        )
        copy.start()
        sent.append(copy)

    def arrived(dst, sem):
        pltpu.make_async_copy(dst, dst, sem).wait()

    def col_slot(owner, chunk):
        return gathered.at[owner, pl.ds(*pieces[chunk])]

    def col_copy(way, step, chunk):
        owner = col + (1 - step if way == 0 else step - 1)
        slot = col_slot(owner, chunk)
        return pltpu.make_async_remote_copy(
            src_ref=column_block.at[pl.ds(*pieces[chunk])] if step == 1 else slot,
            dst_ref=slot,
            send_sem=col_send.at[way, step - 1, chunk],
            recv_sem=col_recv.at[way, step - 1, chunk],
            device_id=after if way == 0 else before,
            device_id_type=MESH,
        )

    def sends(way, step):
        if way == 0:
            return has_after if step == 1 else has_after & (col >= step - 1)
        return has_before if step == 1 else has_before & (col + step - 1 < n_col)

    def takes(way, step):
        return col >= step if way == 0 else col + step < n_col

    def col_own(way):
        @pl.when(sends(way, 1))
        def _():
            for chunk in range(len(pieces)):
                col_copy(way, 1, chunk).start()

    def col_event(step, chunk):
        for way in range(2):
            @pl.when(takes(way, step))
            def _():
                slot = col_slot(col - step if way == 0 else col + step, chunk)
                arrived(slot, col_recv.at[way, step - 1, chunk])

            if step < n_col - 1:
                @pl.when(sends(way, step + 1))
                def _():
                    col_copy(way, step + 1, chunk).start()

    def col_drain():
        for way in range(2):
            for step in range(1, n_col):
                @pl.when(sends(way, step))
                def _():
                    for chunk in range(len(pieces)):
                        col_copy(way, step, chunk).wait_send()

    def strip(offset, lane, chunk):
        owner = chip_at(offset) * 2 + lane
        start = pl.multiple_of(owner * depth, depth)
        return strips.at[pl.ds(start, depth), pl.ds(chunk * wide, wide)]

    def row_send_to(way, step, chunk, src):
        offset = (1 - step) if way == 0 else (step - 1)
        send(
            src, strip(offset, core, chunk),
            row_send.at[way, step - 1, chunk], row_recv.at[way, step - 1, chunk],
            row_next if way == 0 else row_prev,
        )

    def share_strip(offset, chunk, src):
        at = offset + half
        send(
            src, strip(offset, core, chunk),
            sib_send.at[at, chunk], sib_recv.at[at, chunk], sibling,
        )

    shared = [[] for _ in range(ROW_CHUNKS)]

    def row_own(chunk):
        src = row_block.at[:, pl.ds(chunk * wide, wide)]
        for way in range(2):
            if reach(chips, chunk)[way] >= 1:
                row_send_to(way, 1, chunk, src)

    def row_event(step, chunk):
        for way in range(2):
            limit = reach(chips, chunk)[way]
            if step <= limit:
                offset = -step if way == 0 else step
                slot = strip(offset, core, chunk)
                arrived(slot, row_recv.at[way, step - 1, chunk])
                if step < limit:
                    row_send_to(way, step + 1, chunk, slot)
                share_strip(offset, chunk, slot)
                shared[chunk].append(offset)

    def row_shared(chunk):
        for offset in shared[chunk]:
            arrived(strip(offset, 1 - core, chunk), sib_recv.at[offset + half, chunk])

    def make_upper(chunk):
        at = pl.ds(chunk * wide, wide)
        for i in range(order // BLOCK):
            end = (i + 1) * BLOCK
            upper[pl.ds(i * BLOCK, BLOCK), at] = jnp.dot(
                linv[pl.ds(i * BLOCK, BLOCK), pl.ds(0, end)],
                strips[pl.ds(0, end), at],
                preferred_element_type=jnp.float32,
            ).astype(jnp.bfloat16)

    def make_lower(chunk):
        at = pl.ds(*pieces[chunk])
        parts = [gathered[k, at] for k in range(n_col)]
        left = jnp.concatenate(parts, axis=1)
        for j in range(order // BLOCK):
            end = (j + 1) * BLOCK
            lower[at, pl.ds(j * BLOCK, BLOCK)] = jnp.dot(
                left[:, :end],
                uinv[pl.ds(0, end), pl.ds(j * BLOCK, BLOCK)],
                preferred_element_type=jnp.float32,
            ).astype(jnp.bfloat16)
        if share % 128 == 0:
            lower_tile[at] = lower[at, pl.ds(pl.multiple_of(col * share, share), share)]
        else:
            for k in range(n_col):
                @pl.when(col == k)
                def _():
                    lower_tile[at] = lower[at, pl.ds(k * share, share)]
        if chunk == len(pieces) - 1:
            lower_last[...] = lower[at]

    def subtract(chunk):
        at = pl.ds(*pieces[chunk])

        @pl.loop(0, cols // TILE)
        def _(j):
            across = pl.ds(pl.multiple_of(j * TILE, TILE), TILE)
            updated[at, across] -= jnp.dot(
                lower[at], upper[:, across], preferred_element_type=jnp.float32
            )

    col_own(0)
    col_own(1)
    for chunk in range(ROW_CHUNKS):
        row_own(chunk)
    load_t.start()
    pl.when(core == 0)(lambda: pl.semaphore_wait(met, 1))
    for chunk in range(ROW_CHUNKS):
        share_strip(0, chunk, row_block.at[:, pl.ds(chunk * wide, wide)])
        shared[chunk].append(0)
    row_depth = max(max(reach(chips, r)) for r in range(ROW_CHUNKS))
    last = len(pieces) - 1
    for chunk in range(max(len(pieces), ROW_CHUNKS)):
        if chunk < ROW_CHUNKS:
            row_event(1, chunk)
        if chunk <= last:
            col_event(1, chunk)
    for step in range(2, row_depth + 1):
        for chunk in range(ROW_CHUNKS):
            row_event(step, chunk)
    mine_c.wait()
    mine_r.wait()
    load_l.wait()
    load_u.wait()
    for chunk in range(ROW_CHUNKS):
        row_shared(chunk)
        make_upper(chunk)
    load_t.wait()
    for step in range(2, n_col - 1):
        for chunk in range(len(pieces)):
            col_event(step, chunk)
    for chunk in range(len(pieces)):
        col_event(n_col - 1, chunk)
        make_lower(chunk)
        if chunk < last:
            subtract(chunk)
    for copy in sent:
        copy.wait_send()
    col_drain()


def finish(lower_last, lower_done, upper, partial, lower_tile, upper_tile, updated, rest, sem):
    rows, cols = partial.shape
    depth = upper_tile.shape[0]
    start = pl.multiple_of(lax.axis_index("row") * depth, depth)
    pieces = chunks_of(rows)
    at = pl.ds(*pieces[-1])
    copies = [
        pltpu.make_async_copy(partial.at[pl.ds(*piece)], updated.at[pl.ds(*piece)], sem.at[k])
        for k, piece in enumerate(pieces[:-1])
    ]
    copies.append(pltpu.make_async_copy(lower_done, lower_tile, sem.at[len(pieces)]))
    copies.append(
        pltpu.make_async_copy(upper.at[pl.ds(start, depth)], upper_tile, sem.at[len(pieces) + 1])
    )
    for copy in copies:
        copy.start()
    for j in range(cols // BLOCK):
        across = pl.ds(j * BLOCK, BLOCK)
        rest[:, across] = partial[at, across] - jnp.dot(
            lower_last[...], upper[:, across], preferred_element_type=jnp.float32
        )
    tail = pltpu.make_async_copy(rest, updated.at[at], sem.at[len(pieces) - 1])
    tail.start()
    for copy in copies:
        copy.wait()
    tail.wait()


def on_device(n_row, n_col, trailing, column_block, row_block, lower_inv, upper_inv):
    rows, share = column_block.shape
    depth, cols = row_block.shape
    order = lower_inv.shape[0]
    chips = n_row // 2
    hops = chips // 2
    narrow = jnp.bfloat16
    hbm = pl.BlockSpec(memory_space=pltpu.HBM)
    inside = pl.BlockSpec(memory_space=pltpu.VMEM)
    dma = pltpu.SemaphoreType.DMA
    count = len(PARTS)
    last = chunks_of(rows)[-1][1]
    inputs = (trailing, column_block, row_block, lower_inv, upper_inv)
    tile = jax.ShapeDtypeStruct((rows, share), narrow)
    whole = jax.ShapeDtypeStruct((rows, cols), jnp.float32)
    lower_done, lower_last, upper, partial = pl.pallas_call(
        functools.partial(kernel, n_row, n_col),
        out_shape=(
            tile,
            jax.ShapeDtypeStruct((last, order), narrow),
            jax.ShapeDtypeStruct((order, cols), narrow),
            whole,
        ),
        in_specs=[hbm] * 5,
        out_specs=(inside,) * 4,
        scratch_shapes=[
            pltpu.VMEM((n_col, rows, share), narrow),
            pltpu.VMEM((order, cols), narrow),
            pltpu.VMEM((order, order), narrow),
            pltpu.VMEM((order, order), narrow),
            pltpu.VMEM((rows, order), narrow),
            dma((3,)),
            dma((2,)),
            dma((2, n_col - 1, count)),
            dma((2, n_col - 1, count)),
            dma((2, hops, ROW_CHUNKS)),
            dma((2, hops, ROW_CHUNKS)),
            dma((2 * hops + 1, ROW_CHUNKS)),
            dma((2 * hops + 1, ROW_CHUNKS)),
            pltpu.SemaphoreType.REGULAR,
        ],
        compiler_params=pltpu.CompilerParams(
            collective_id=0, has_side_effects=True, vmem_limit_bytes=32 << 20
        ),
    )(*(pltpu.with_memory_space_constraint(x, pltpu.HBM) for x in inputs))
    return pl.pallas_call(
        finish,
        out_shape=(tile, jax.ShapeDtypeStruct((depth, cols), narrow), whole),
        in_specs=[inside] * 4,
        out_specs=(hbm,) * 3,
        scratch_shapes=[pltpu.VMEM((last, cols), jnp.float32), dma((count + 2,))],
        compiler_params=pltpu.CompilerParams(vmem_limit_bytes=16 << 20),
    )(lower_last, lower_done, upper, partial)


def solution(mesh):
    specs = P("row", "col")
    return jax.shard_map(
        functools.partial(on_device, mesh.shape["row"], mesh.shape["col"]),
        mesh=mesh,
        in_specs=(specs, specs, specs, P(), P()),
        out_specs=(specs,) * 3,
        check_vma=False,
    )
```

```python
import functools

import jax
import jax.numpy as jnp
from jax import lax
from jax.experimental import pallas as pl
from jax.experimental.pallas import tpu as pltpu
from jax.sharding import PartitionSpec as P

MESH = pl.DeviceIdType.MESH
BLOCK = 256
PARTS = (3, 3, 3, 3)
ROW_CHUNKS = 4


def chunks_of(rows):
    unit = rows // sum(PARTS)
    starts = [sum(PARTS[:k]) * unit for k in range(len(PARTS))]
    return [(start, part * unit) for start, part in zip(starts, PARTS)]


def reach(size, chunk):
    each = (size - 1) // 2
    extra = 1 if size % 2 == 0 else 0
    return (each + extra, each) if chunk % 2 == 0 else (each, each + extra)


def kernel(
    n_row, n_col,
    trailing, column_block, row_block, lower_inv, upper_inv,
    lower_tile, lower_last, upper, updated,
    gathered, strips, linv, uinv, lower,
    local_sem, own_sem, col_send, col_recv, row_send, row_recv, sib_send, sib_recv, met,
):
    rows, share = column_block.shape
    depth, cols = row_block.shape
    order = lower_inv.shape[0]
    pieces = chunks_of(rows)
    wide = cols // ROW_CHUNKS
    row, col = lax.axis_index("row"), lax.axis_index("col")
    chips = n_row // 2
    half = chips // 2
    core = lax.rem(row, 2)

    def snake(place):
        return place + (place // half) * (chips + half - 1 - 2 * place)

    place = snake(row // 2)

    def chip_at(offset):
        return snake(lax.rem(place + chips + offset, chips))

    sibling = {"row": row + 1 - 2 * core}
    row_next = {"row": chip_at(1) * 2 + core}
    row_prev = {"row": chip_at(-1) * 2 + core}
    after = {"col": col + 1}
    before = {"col": col - 1}
    has_after = col < n_col - 1
    has_before = col > 0

    load_l = pltpu.make_async_copy(lower_inv, linv, local_sem.at[0])
    load_u = pltpu.make_async_copy(upper_inv, uinv, local_sem.at[1])
    load_t = pltpu.make_async_copy(trailing, updated, local_sem.at[2])
    mine_c = pltpu.make_async_copy(column_block, gathered.at[col], own_sem.at[0])
    my_rows = pl.ds(pl.multiple_of(row * depth, depth), depth)
    mine_r = pltpu.make_async_copy(row_block, strips.at[my_rows], own_sem.at[1])

    barrier = pltpu.get_barrier_semaphore()

    def greet(device):
        pl.semaphore_signal(barrier, inc=1, device_id=device, device_id_type=MESH)

    pl.when(has_after)(lambda: greet(after))
    pl.when(has_before)(lambda: greet(before))
    greet(row_next)
    greet(row_prev)
    pl.when(core == 0)(lambda: greet(sibling))
    mine_c.start()
    mine_r.start()
    load_l.start()
    load_u.start()
    ahead = (2 * n_col - 3 - col) // (n_col - 1)
    behind = (n_col - 2 + col) // (n_col - 1)
    pl.semaphore_wait(barrier, 2 + core + ahead + behind)

    @pl.when(core == 1)
    def _():
        pl.semaphore_signal(met, inc=1, device_id=sibling, device_id_type=MESH)


    sent = []

    def send(src, dst, send_sem, recv_sem, device):
        copy = pltpu.make_async_remote_copy(
            src_ref=src, dst_ref=dst, send_sem=send_sem, recv_sem=recv_sem,
            device_id=device, device_id_type=MESH,
        )
        copy.start()
        sent.append(copy)

    def arrived(dst, sem):
        pltpu.make_async_copy(dst, dst, sem).wait()

    def col_slot(owner, chunk):
        return gathered.at[owner, pl.ds(*pieces[chunk])]

    def col_copy(way, step, chunk):
        owner = col + (1 - step if way == 0 else step - 1)
        slot = col_slot(owner, chunk)
        return pltpu.make_async_remote_copy(
            src_ref=column_block.at[pl.ds(*pieces[chunk])] if step == 1 else slot,
            dst_ref=slot,
            send_sem=col_send.at[way, step - 1, chunk],
            recv_sem=col_recv.at[way, step - 1, chunk],
            device_id=after if way == 0 else before,
            device_id_type=MESH,
        )

    def sends(way, step):
        if way == 0:
            return has_after if step == 1 else has_after & (col >= step - 1)
        return has_before if step == 1 else has_before & (col + step - 1 < n_col)

    def takes(way, step):
        return col >= step if way == 0 else col + step < n_col

    def col_own(way):
        @pl.when(sends(way, 1))
        def _():
            for chunk in range(len(pieces)):
                col_copy(way, 1, chunk).start()

    def col_event(step, chunk):
        for way in range(2):
            @pl.when(takes(way, step))
            def _():
                slot = col_slot(col - step if way == 0 else col + step, chunk)
                arrived(slot, col_recv.at[way, step - 1, chunk])

            if step < n_col - 1:
                @pl.when(sends(way, step + 1))
                def _():
                    col_copy(way, step + 1, chunk).start()

    def col_drain():
        for way in range(2):
            for step in range(1, n_col):
                @pl.when(sends(way, step))
                def _():
                    for chunk in range(len(pieces)):
                        col_copy(way, step, chunk).wait_send()

    def strip(offset, lane, chunk):
        owner = chip_at(offset) * 2 + lane
        start = pl.multiple_of(owner * depth, depth)
        return strips.at[pl.ds(start, depth), pl.ds(chunk * wide, wide)]

    def row_send_to(way, step, chunk, src):
        offset = (1 - step) if way == 0 else (step - 1)
        send(
            src, strip(offset, core, chunk),
            row_send.at[way, step - 1, chunk], row_recv.at[way, step - 1, chunk],
            row_next if way == 0 else row_prev,
        )

    def share_strip(offset, chunk, src):
        at = offset + half
        send(
            src, strip(offset, core, chunk),
            sib_send.at[at, chunk], sib_recv.at[at, chunk], sibling,
        )

    shared = [[] for _ in range(ROW_CHUNKS)]

    def row_own(chunk):
        src = row_block.at[:, pl.ds(chunk * wide, wide)]
        for way in range(2):
            if reach(chips, chunk)[way] >= 1:
                row_send_to(way, 1, chunk, src)

    def row_event(step, chunk):
        for way in range(2):
            limit = reach(chips, chunk)[way]
            if step <= limit:
                offset = -step if way == 0 else step
                slot = strip(offset, core, chunk)
                arrived(slot, row_recv.at[way, step - 1, chunk])
                if step < limit:
                    row_send_to(way, step + 1, chunk, slot)
                share_strip(offset, chunk, slot)
                shared[chunk].append(offset)

    def row_shared(chunk):
        for offset in shared[chunk]:
            arrived(strip(offset, 1 - core, chunk), sib_recv.at[offset + half, chunk])

    def make_upper(chunk):
        at = pl.ds(chunk * wide, wide)
        for i in range(order // BLOCK):
            end = (i + 1) * BLOCK
            upper[pl.ds(i * BLOCK, BLOCK), at] = jnp.dot(
                linv[pl.ds(i * BLOCK, BLOCK), pl.ds(0, end)],
                strips[pl.ds(0, end), at],
                preferred_element_type=jnp.float32,
            ).astype(jnp.bfloat16)

    def make_lower(chunk):
        at = pl.ds(*pieces[chunk])
        parts = [gathered[k, at] for k in range(n_col)]
        left = jnp.concatenate(parts, axis=1)
        for j in range(order // BLOCK):
            end = (j + 1) * BLOCK
            lower[at, pl.ds(j * BLOCK, BLOCK)] = jnp.dot(
                left[:, :end],
                uinv[pl.ds(0, end), pl.ds(j * BLOCK, BLOCK)],
                preferred_element_type=jnp.float32,
            ).astype(jnp.bfloat16)
        if share % 128 == 0:
            lower_tile[at] = lower[at, pl.ds(pl.multiple_of(col * share, share), share)]
        else:
            for k in range(n_col):
                @pl.when(col == k)
                def _():
                    lower_tile[at] = lower[at, pl.ds(k * share, share)]
        if chunk == len(pieces) - 1:
            lower_last[...] = lower[at]

    def subtract(chunk):
        at = pl.ds(*pieces[chunk])
        updated[at] -= jnp.dot(lower[at], upper[...], preferred_element_type=jnp.float32)

    col_own(0)
    col_own(1)
    for chunk in range(ROW_CHUNKS):
        row_own(chunk)
    load_t.start()
    pl.when(core == 0)(lambda: pl.semaphore_wait(met, 1))
    for chunk in range(ROW_CHUNKS):
        share_strip(0, chunk, row_block.at[:, pl.ds(chunk * wide, wide)])
        shared[chunk].append(0)
    row_depth = max(max(reach(chips, r)) for r in range(ROW_CHUNKS))
    last = len(pieces) - 1
    for chunk in range(max(len(pieces), ROW_CHUNKS)):
        if chunk < ROW_CHUNKS:
            row_event(1, chunk)
        if chunk <= last:
            col_event(1, chunk)
    for step in range(2, row_depth + 1):
        for chunk in range(ROW_CHUNKS):
            row_event(step, chunk)
    mine_c.wait()
    mine_r.wait()
    load_l.wait()
    load_u.wait()
    for chunk in range(ROW_CHUNKS):
        row_shared(chunk)
        make_upper(chunk)
    load_t.wait()
    for step in range(2, n_col - 1):
        for chunk in range(len(pieces)):
            col_event(step, chunk)
    for chunk in range(len(pieces)):
        col_event(n_col - 1, chunk)
        if chunk == last:
            for copy in sent:
                copy.wait_send()
            col_drain()
        make_lower(chunk)
        if chunk < last:
            subtract(chunk)


def finish(lower_last, lower_done, upper, partial, lower_tile, upper_tile, updated, rest, sem):
    rows, cols = partial.shape
    depth = upper_tile.shape[0]
    start = pl.multiple_of(lax.axis_index("row") * depth, depth)
    pieces = chunks_of(rows)
    at = pl.ds(*pieces[-1])
    copies = [
        pltpu.make_async_copy(partial.at[pl.ds(*piece)], updated.at[pl.ds(*piece)], sem.at[k])
        for k, piece in enumerate(pieces[:-1])
    ]
    copies.append(pltpu.make_async_copy(lower_done, lower_tile, sem.at[len(pieces)]))
    copies.append(
        pltpu.make_async_copy(upper.at[pl.ds(start, depth)], upper_tile, sem.at[len(pieces) + 1])
    )
    for copy in copies:
        copy.start()
    for j in range(cols // BLOCK):
        across = pl.ds(j * BLOCK, BLOCK)
        rest[:, across] = partial[at, across] - jnp.dot(
            lower_last[...], upper[:, across], preferred_element_type=jnp.float32
        )
    tail = pltpu.make_async_copy(rest, updated.at[at], sem.at[len(pieces) - 1])
    tail.start()
    for copy in copies:
        copy.wait()
    tail.wait()


def on_device(n_row, n_col, trailing, column_block, row_block, lower_inv, upper_inv):
    rows, share = column_block.shape
    depth, cols = row_block.shape
    order = lower_inv.shape[0]
    chips = n_row // 2
    hops = chips // 2
    narrow = jnp.bfloat16
    hbm = pl.BlockSpec(memory_space=pltpu.HBM)
    inside = pl.BlockSpec(memory_space=pltpu.VMEM)
    dma = pltpu.SemaphoreType.DMA
    count = len(PARTS)
    last = chunks_of(rows)[-1][1]
    inputs = (trailing, column_block, row_block, lower_inv, upper_inv)
    tile = jax.ShapeDtypeStruct((rows, share), narrow)
    whole = jax.ShapeDtypeStruct((rows, cols), jnp.float32)
    lower_done, lower_last, upper, partial = pl.pallas_call(
        functools.partial(kernel, n_row, n_col),
        out_shape=(
            tile,
            jax.ShapeDtypeStruct((last, order), narrow),
            jax.ShapeDtypeStruct((order, cols), narrow),
            whole,
        ),
        in_specs=[hbm] * 5,
        out_specs=(inside,) * 4,
        scratch_shapes=[
            pltpu.VMEM((n_col, rows, share), narrow),
            pltpu.VMEM((order, cols), narrow),
            pltpu.VMEM((order, order), narrow),
            pltpu.VMEM((order, order), narrow),
            pltpu.VMEM((rows, order), narrow),
            dma((3,)),
            dma((2,)),
            dma((2, n_col - 1, count)),
            dma((2, n_col - 1, count)),
            dma((2, hops, ROW_CHUNKS)),
            dma((2, hops, ROW_CHUNKS)),
            dma((2 * hops + 1, ROW_CHUNKS)),
            dma((2 * hops + 1, ROW_CHUNKS)),
            pltpu.SemaphoreType.REGULAR,
        ],
        compiler_params=pltpu.CompilerParams(
            collective_id=0, has_side_effects=True, vmem_limit_bytes=32 << 20
        ),
    )(*(pltpu.with_memory_space_constraint(x, pltpu.HBM) for x in inputs))
    return pl.pallas_call(
        finish,
        out_shape=(tile, jax.ShapeDtypeStruct((depth, cols), narrow), whole),
        in_specs=[inside] * 4,
        out_specs=(hbm,) * 3,
        scratch_shapes=[pltpu.VMEM((last, cols), jnp.float32), dma((count + 2,))],
        compiler_params=pltpu.CompilerParams(vmem_limit_bytes=16 << 20),
    )(lower_last, lower_done, upper, partial)


def solution(mesh):
    specs = P("row", "col")
    return jax.shard_map(
        functools.partial(on_device, mesh.shape["row"], mesh.shape["col"]),
        mesh=mesh,
        in_specs=(specs, specs, specs, P(), P()),
        out_specs=(specs,) * 3,
        check_vma=False,
    )
```
